256 devices in a mesh: wide: 64 (over x, z, core), narrow: 4 (over y).
Axes of the slice: x: 4, y: 4, z: 8, core: 2. Of those that a mesh axis runs over, the one named last changes fastest.
Arguments:
- dosage: bfloat16 [262144, 4096], P(('wide', 'narrow')), may hold values from 0 to 2
- keep_rows: int32 [229376], P(('wide', 'narrow')), may hold values from 0 to 1023, as said below
- allele_counts: int32 [4096], replicated, may hold values from 157286 to 367000, as said below
- projection: bfloat16 [4096, 128], replicated, may hold values from -0.09375 to 0.09375
Outputs:
- scores: float32 [229376, 128], P(('wide', 'narrow'))
- loadings: float32 [4096, 128], P('narrow')
The draws below stay inside these ranges and needn't reach their ends.
Inputs may be any that keep to these rules, and one draw needn't show every extreme that they name: `keep_rows`: each block of 896 entries holds distinct local row numbers of one device's 1024 samples, ascending. `allele_counts`: totals over all 262144 genotyped samples, before outlier removal.
All inputs are finite; a program needn't handle non-finite values.
Results may differ from the reference program's by a relative error of at most 0.0075.
The reference program's roundings to bfloat16 on the way count: a program that leaves them out, or rounds other values in their place, can miss the bound.
Values sent between devices are 32-bit elements; how exact they have to be, the bound alone decides.
A program may use at most 64 MiB of HBM per device.

```python
import math
import jax
import jax.numpy as jnp
from jax import lax

SNPS = 4096
COMPONENTS = 128
ITERS = 2
SAMP_DEV = 1024
KEEP_DEV = 896
BLOCKS = 256
NARROW_BLOCKS = 4
SAMPLES = 262144
KEPT = 229376


def allele_draw(key):
    lowest = 3 * SAMPLES // 5
    highest = 7 * SAMPLES // 5
    counts_base = jax.random.randint(jax.random.fold_in(key, 11), (SNPS,), lowest, highest)
    first_slot = jax.random.randint(jax.random.fold_in(key, 12), (), 0, SNPS)
    shift_by = jax.random.randint(jax.random.fold_in(key, 13), (), 1, SNPS)
    second_slot = (first_slot + shift_by) % SNPS
    counts_base = counts_base.at[first_slot].set(lowest)
    counts_base = counts_base.at[second_slot].set(highest - 1)
    return counts_base.astype(jnp.int32)


def draw_allele_counts(key, part):
    return allele_draw(key)


def draw_dosage(key, part):
    counts = allele_draw(key)
    frequency = counts.astype(jnp.float32) / (2.0 * SAMPLES)
    noise_field = jnp.clip(0.5 * jax.random.normal(jax.random.fold_in(key, 22), (SAMPLES, SNPS), jnp.float32), -1.0, 1.0)
    block_index = jnp.arange(SAMPLES) // SAMP_DEV
    wide_pos = (block_index // NARROW_BLOCKS).astype(jnp.float32)
    narrow_pos = (block_index % NARROW_BLOCKS).astype(jnp.float32)
    wide_count = BLOCKS // NARROW_BLOCKS
    wide_frac = wide_pos / (wide_count - 1)
    narrow_frac = narrow_pos / (NARROW_BLOCKS - 1)
    power = (1.0 + wide_frac + narrow_frac) / 3.0
    amplitude = 0.6 * jnp.sqrt(power)
    values = 2.0 * frequency[None, :] + amplitude[:, None] * noise_field
    factors = 8
    sample_factors = jnp.clip(jax.random.normal(jax.random.fold_in(key, 41), (SAMPLES, factors), jnp.float32), -3.0, 3.0)
    snp_factors = jnp.clip(jax.random.normal(jax.random.fold_in(key, 42), (factors, SNPS), jnp.float32), -3.0, 3.0)
    for factor in range(factors):
        strength = 1.2 * 0.85 ** factor / math.sqrt(SNPS)
        values = values + sample_factors[:, factor][:, None] * (strength * snp_factors[factor])[None, :]
    return jnp.clip(values, 0.0, 2.0).astype(jnp.bfloat16)


def draw_keep_rows(key, part):
    block_keys = jax.random.split(jax.random.fold_in(key, 31), BLOCKS)

    def choose_rows(one_key):
        return jnp.sort(jax.random.permutation(one_key, SAMP_DEV)[:KEEP_DEV])
    return jax.vmap(choose_rows)(block_keys).reshape(KEPT).astype(jnp.int32)


def normal_values(own_key, dims, deviation, most, kind=jnp.bfloat16):
    return jnp.clip(deviation * jax.random.normal(own_key, dims, jnp.float32), -most, most).astype(kind)


def setup_inputs(seed: int = 0) -> dict:
    splits = jax.random.split(jax.random.key(seed), 5)
    dosage = draw_dosage(jax.random.fold_in(splits[4], 71), 0)
    keep_rows = draw_keep_rows(jax.random.fold_in(splits[4], 71), 0)
    allele_counts = draw_allele_counts(jax.random.fold_in(splits[4], 71), 0)
    projection = normal_values(splits[3], (SNPS, COMPONENTS), SNPS ** -0.5, 0.09375)
    return {"dosage": dosage, "keep_rows": keep_rows, "allele_counts": allele_counts, "projection": projection}


def standardize(dosage, keep_rows, allele_counts):
    frequency = allele_counts.astype(jnp.float32) / (2.0 * SAMPLES)
    center = 2.0 * frequency
    spread = jnp.sqrt(2.0 * frequency * (1.0 - frequency))
    blocks = dosage.reshape(BLOCKS, SAMP_DEV, SNPS)
    picks = keep_rows.reshape(BLOCKS, KEEP_DEV)

    def one_block(pair):
        block_rows, pick_rows = pair
        chosen = jnp.take(block_rows, pick_rows, axis=0)
        return ((chosen.astype(jnp.float32) - center) / spread).astype(jnp.bfloat16)
    return lax.map(one_block, (blocks, picks)).reshape(KEPT, SNPS)

def invert_factor(gram_matrix):
    lower_factor = jnp.linalg.cholesky(gram_matrix)
    unit_matrix = jnp.eye(gram_matrix.shape[0], dtype=jnp.float32)
    return jax.scipy.linalg.solve_triangular(lower_factor, unit_matrix, lower=True)

def reference(dosage, keep_rows, allele_counts, projection):
    standard = standardize(dosage, keep_rows, allele_counts)
    basis_bf = projection
    projected = None
    inverse = None
    loadings = None
    for iteration in range(ITERS):
        projected = jnp.dot(standard.astype(jnp.float32), basis_bf.astype(jnp.float32), preferred_element_type=jnp.float32).astype(jnp.bfloat16)
        gram_matrix = jnp.dot(projected.T.astype(jnp.float32), projected.astype(jnp.float32), preferred_element_type=jnp.float32)
        inverse = invert_factor(gram_matrix)
        partial_value = jnp.dot(standard.T.astype(jnp.float32), projected.astype(jnp.float32), preferred_element_type=jnp.float32)
        loadings = jnp.dot(partial_value, inverse.T, precision=lax.Precision.HIGHEST)
        basis_bf = loadings.astype(jnp.bfloat16)
    scores = jnp.dot(projected.astype(jnp.float32), inverse.T, precision=lax.Precision.HIGHEST) * math.sqrt(KEPT)
    return (scores, loadings)
```

```python
import math

import jax
import jax.numpy as jnp
from jax import lax
from jax.experimental import pallas as pl
from jax.experimental.pallas import tpu as pltpu
from jax.sharding import PartitionSpec as P

ITERS = 2
NX, NY, NZ = 4, 4, 8
COMP = 128
SLAB = 512
MESH = pl.DeviceIdType.MESH
HIGH = lax.Precision.HIGHEST

PER_ITER = 46


def kernel(
    samples_total,
    kept_total,
    dosage_hbm,
    keep_ref,
    counts_ref,
    proj_ref,
    scores_ref,
    load_ref,
    stand,
    acc,
    pm,
    pt,
    mask,
    wt,
    core_in,
    chip_sum,
    first_in,
    first_sum,
    second_in,
    second_sum,
    third_in,
    whole,
    basis_t,
    gram,
    gram_core,
    gram_half,
    gram_x,
    gram_y,
    gram_z,
    gram_all,
    elim,
    unit,
    inv_t,
    kept,
    load_sem,
    send_sem,
    recv_sem,
):
    wide = lax.axis_index("wide")
    y = lax.axis_index("narrow")
    c = lax.rem(wide, 2)
    z = lax.rem(lax.div(wide, 2), NZ)
    x = lax.div(wide, 2 * NZ)
    f = x * (1 - c) + y * c
    s = y * (1 - c) + x * c

    def at(px, py, pz, pc):
        return ((px * NZ + pz) * 2 + pc, py)

    partner = at(x, y, z, 1 - c)

    def along_x(k):
        return at(lax.rem(x + k, NX), y, z, c)

    def along_y(k):
        return at(x, lax.rem(y + k, NY), z, c)

    def along_z(k):
        return at(x, y, lax.rem(z + k, NZ), c)

    def along_f(k):
        return at(lax.rem(x + k * (1 - c), NX), lax.rem(y + k * c, NY), z, c)

    def along_s(k):
        return at(lax.rem(x + k * c, NX), lax.rem(y + k * (1 - c), NY), z, c)

    snps = stand.shape[1]
    slabs = snps // SLAB

    loads = []
    for i in range(slabs):
        part = pl.ds(i * SLAB, SLAB)
        loads.append(
            pltpu.make_async_copy(
                dosage_hbm.at[:, part], stand.at[:, part], load_sem.at[i]
            )
        )
        loads[-1].start()

    barrier = pltpu.get_barrier_semaphore()
    others = (
        [partner]
        + [along_x(k) for k in range(1, NX)]
        + [along_y(k) for k in range(1, NY)]
        + [along_z(k) for k in range(1, NZ)]
    )
    for other in others:
        pl.semaphore_signal(barrier, inc=1, device_id=other, device_id_type=MESH)

    keep_row = keep_ref[...]
    rows = stand.shape[0]
    n_kept = keep_row.shape[1]

    @pl.loop(0, rows // 128)
    def _(i):
        ids = lax.broadcasted_iota(jnp.int32, (128, n_kept), 0) + i * 128
        hit = jnp.max(
            jnp.where(ids == keep_row, 1.0, 0.0), axis=1, keepdims=True
        )
        mask[pl.ds(i * 128, 128), :] = jnp.broadcast_to(hit, (128, COMP))

    frequency = counts_ref[...].astype(jnp.float32) / (2.0 * samples_total)
    center = 2.0 * frequency
    scale = 1.0 / jnp.sqrt(2.0 * frequency * (1.0 - frequency))

    for i in range(slabs):
        loads[i].wait()
        part = slice(i * SLAB, (i + 1) * SLAB)
        mid = center[:, part]
        mul = scale[:, part]

        @pl.loop(0, rows // 64)
        def _(r):
            here = pl.ds(r * 64, 64)
            raw = stand[here, part].astype(jnp.float32)
            stand[here, part] = ((raw - mid) * mul).astype(jnp.bfloat16)

        term = jnp.dot(
            stand[:, part], proj_ref[part, :], preferred_element_type=jnp.float32
        )
        if i == 0:
            acc[...] = term
        else:
            acc[...] += term

    pl.semaphore_wait(barrier, len(others))

    sent = []
    count = [0]

    def send(src, dst, device):
        copy = pltpu.make_async_remote_copy(
            src_ref=src,
            dst_ref=dst,
            send_sem=send_sem.at[count[0]],
            recv_sem=recv_sem.at[count[0]],
            device_id=device,
            device_id_type=MESH,
        )
        count[0] += 1
        copy.start()
        sent.append(copy)
        return copy

    def arrive(copies):
        for copy in copies:
            copy.wait_recv()

    def eliminate(low, high):
        @pl.loop(low, high)
        def _(j):
            lane = lax.broadcasted_iota(jnp.int32, (COMP, COMP), 1)
            sub = lax.broadcasted_iota(jnp.int32, (COMP, 1), 0)
            lane_row = lax.broadcasted_iota(jnp.int32, (1, COMP), 1)
            now = elim[...]
            column = jnp.sum(jnp.where(lane == j, now, 0.0), axis=1, keepdims=True)
            row = elim[pl.ds(j, 1), :]
            unit_row = unit[pl.ds(j, 1), :]
            pivot = jnp.sum(
                jnp.where(lane_row == j, row, 0.0), axis=1, keepdims=True
            )
            factor = jnp.where(sub > j, column / pivot, 0.0)
            elim[...] = now - factor * row
            unit[...] = unit[...] - factor * unit_row

    for t in range(ITERS):
        last = t + 1 == ITERS
        wt_t, core_t, chip_t = wt.at[t], core_in.at[t], chip_sum.at[t]
        whole_t = whole.at[t]

        @pl.loop(0, rows // 128)
        def _(i):
            here = pl.ds(pl.multiple_of(i * 128, 128), 128)
            value = jnp.where(mask[here, :] > 0.0, acc[here, :], 0.0)
            pm[here, :] = value.astype(jnp.bfloat16)
            pt[:, here] = value.T.astype(jnp.bfloat16)

        gram[t] = jnp.dot(pt[...], pm[...], preferred_element_type=jnp.float32)
        g_core = send(gram.at[t], gram_core.at[t], partner)

        def partial_of(which):
            @pl.loop(0, NY)
            def _(i):
                start = pl.multiple_of(i * (snps // NY) + which * SLAB, SLAB)
                value = jnp.dot(
                    pt[...],
                    stand[:, pl.ds(start, SLAB)],
                    preferred_element_type=jnp.float32,
                )
                for j in range(NX):
                    pf = j * (1 - which) + i * which
                    ps = i * (1 - which) + j * which
                    wt_t[which, pf, ps] = value[:, j * 128 : (j + 1) * 128]

        partial_of(1 - c)
        core = send(wt_t.at[1 - c], core_t, partner)

        arrive([g_core])
        half = pl.ds(pl.multiple_of(c * 64, 64), 64)
        gram_half[t] = gram[t, half, :] + gram_core[t, half, :]
        g_x = []
        for k in range(1, NX):
            to = lax.rem(x + k, NX)
            g_x.append(
                send(
                    gram_half.at[t, pl.ds(pl.multiple_of(to * 16, 16), 16), :],
                    gram_x.at[t, x],
                    along_x(k),
                )
            )
        gram_x[t, x] = gram_half[t, pl.ds(pl.multiple_of(x * 16, 16), 16), :]

        partial_of(c)
        arrive([core])
        for i in range(4):

            @pl.loop(0, 4)
            def _(j):
                chip_t[i, j] = wt_t[c, i, j] + core_t[i, j]

        first = []
        for k in range(1, 4):
            to = lax.rem(f + k, 4)
            first.append(send(chip_t.at[to], first_in.at[t, k - 1], along_f(k)))

        arrive(g_x)
        gram_y[t, y] = (
            (gram_x[t, 0] + gram_x[t, 1]) + gram_x[t, 2]
        ) + gram_x[t, 3]
        g_y = [
            send(gram_y.at[t, y], gram_y.at[t, y], along_y(k)) for k in range(1, NY)
        ]
        arrive(g_y)
        gram_z[t, z] = (
            (gram_y[t, 0] + gram_y[t, 1]) + gram_y[t, 2]
        ) + gram_y[t, 3]
        g_z = [
            send(gram_z.at[t, z], gram_z.at[t, z], along_z(k)) for k in range(1, NZ)
        ]

        arrive(first)

        @pl.loop(0, 4)
        def _(j):
            first_sum[t, j] = (
                (chip_t[f, j] + first_in[t, 0, j]) + first_in[t, 1, j]
            ) + first_in[t, 2, j]

        second = []
        for k in range(1, 4):
            to = lax.rem(s + k, 4)
            second.append(
                send(first_sum.at[t, to], second_in.at[t, k - 1], along_s(k))
            )

        arrive(g_z)
        total = gram_z[t, 0]
        for k in range(1, NZ):
            total = total + gram_z[t, k]
        mine = pl.ds(pl.multiple_of(c * 64 + x * 16, 16), 16)
        gram_all[t, mine, :] = total
        g_xa = [
            send(gram_all.at[t, mine, :], gram_all.at[t, mine, :], along_x(k))
            for k in range(1, NX)
        ]

        arrive(second)
        second_sum[t] = (
            (first_sum[t, s] + second_in[t, 0]) + second_in[t, 1]
        ) + second_in[t, 2]
        third = []
        for k in range(1, NZ):
            to = lax.rem(z + k, NZ)
            third.append(
                send(
                    second_sum.at[t, pl.ds(pl.multiple_of(to * 16, 16), 16), :],
                    third_in.at[t, k - 1],
                    along_z(k),
                )
            )

        arrive(g_xa)
        g_ca = send(gram_all.at[t, half, :], gram_all.at[t, half, :], partner)
        arrive([g_ca])
        elim[...] = gram_all[t]
        unit[...] = jnp.where(
            lax.broadcasted_iota(jnp.int32, (COMP, COMP), 0)
            == lax.broadcasted_iota(jnp.int32, (COMP, COMP), 1),
            1.0,
            0.0,
        )

        arrive(third)
        piece = pl.ds(pl.multiple_of(z * 16, 16), 16)
        own = second_sum[t, piece, :]
        for k in range(1, NZ):
            own = own + third_in[t, k - 1]
        whole_t[c, f, s, piece, :] = own
        out_z = [
            send(
                whole_t.at[c, f, s, piece, :],
                whole_t.at[c, f, s, piece, :],
                along_z(k),
            )
            for k in range(1, NZ)
        ]
        eliminate(0, 40)
        arrive(out_z)
        block = whole_t.at[c, f, s]
        if not last:
            out_s = [send(block, block, along_s(k)) for k in range(1, 4)]
            eliminate(40, 72)
            arrive(out_s)
            band = whole_t.at[c, f]
            out_f = [send(band, band, along_f(k)) for k in range(1, 4)]
            eliminate(72, 128)
            arrive(out_f)
            out_c = send(whole_t.at[c], whole_t.at[c], partner)
        else:
            out_s = [send(block, block, along_x(k)) for k in range(1, 4)]
            eliminate(40, 72)
            arrive(out_s)
            out_c = None

        if last:
            pairs = []
            for k in range(NX):
                pf = k * (1 - c) + y * c
                ps = y * (1 - c) + k * c
                ref = whole_t.at[c, pf, ps]
                pairs.append(send(ref, ref, partner))
            eliminate(72, 128)

        diagonal = jnp.sum(
            jnp.where(
                lax.broadcasted_iota(jnp.int32, (COMP, COMP), 0)
                == lax.broadcasted_iota(jnp.int32, (COMP, COMP), 1),
                elim[...],
                0.0,
            ),
            axis=1,
            keepdims=True,
        )
        inverse = unit[...] * (1.0 / jnp.sqrt(diagonal))
        unit[...] = inverse
        inv_t[...] = inverse.T

        if not last:
            arrive([out_c])
            for pc in range(2):
                for pf in range(4):
                    for ps in range(4):
                        px, py = (pf, ps) if pc == 0 else (ps, pf)
                        col = (py * 8 + pc * 4 + px) * 128
                        value = jnp.dot(
                            unit[...],
                            whole_t[pc, pf, ps],
                            precision=HIGH,
                            preferred_element_type=jnp.float32,
                        )
                        basis_t[:, col : col + 128] = value.astype(jnp.bfloat16)
            for i in range(slabs):
                part = slice(i * SLAB, (i + 1) * SLAB)
                term = lax.dot_general(
                    stand[:, part],
                    basis_t[:, part],
                    (((1,), (1,)), ((), ())),
                    preferred_element_type=jnp.float32,
                )
                if i == 0:
                    acc[...] = term
                else:
                    acc[...] += term
        else:
            root = math.sqrt(kept_total)

            @pl.loop(0, n_kept // 128)
            def _(i):
                here = pl.ds(pl.multiple_of(i * 128, 128), 128)
                picks = jnp.broadcast_to(keep_ref[:, here], (128, 128)).T
                lane = lax.broadcasted_iota(jnp.int32, (128, 128), 1)
                one_hot = jnp.concatenate(
                    [
                        jnp.where(picks == lane + 128 * k, 1.0, 0.0).astype(
                            jnp.bfloat16
                        )
                        for k in range(rows // 128)
                    ],
                    axis=1,
                )
                chosen = jnp.dot(
                    one_hot, pm[...], preferred_element_type=jnp.float32
                )
                scores_ref[here, :] = (
                    jnp.dot(
                        chosen,
                        inv_t[...],
                        precision=HIGH,
                        preferred_element_type=jnp.float32,
                    )
                    * root
                )

            arrive(pairs)
            for pc in range(2):
                for k in range(NX):
                    if pc == 0:
                        value = whole_t[0, k, y]
                    else:
                        value = whole_t[1, y, k]
                    value = jnp.dot(
                        unit[...],
                        value,
                        precision=HIGH,
                        preferred_element_type=jnp.float32,
                    )
                    row0 = (pc * NX + k) * 128
                    load_ref[row0 : row0 + 128, :] = value.T

    for copy in sent:
        copy.wait_send()


def on_device(dosage, keep_rows, allele_counts, projection):
    groups = lax.axis_size("wide") * lax.axis_size("narrow")
    rows, snps = dosage.shape
    n_kept = keep_rows.shape[0]
    share = snps // lax.axis_size("narrow")
    f32, bf16 = jnp.float32, jnp.bfloat16
    vmem = pltpu.VMEM
    total_copies = 49 * ITERS

    def body(*refs):
        kernel(rows * groups, n_kept * groups, *refs)

    return pl.pallas_call(
        body,
        out_shape=(
            jax.ShapeDtypeStruct((n_kept, COMP), f32),
            jax.ShapeDtypeStruct((share, COMP), f32),
        ),
        in_specs=[
            pl.BlockSpec(memory_space=pl.ANY),
            pl.BlockSpec(memory_space=vmem),
            pl.BlockSpec(memory_space=vmem),
            pl.BlockSpec(memory_space=vmem),
        ],
        out_specs=(
            pl.BlockSpec(memory_space=vmem),
            pl.BlockSpec(memory_space=vmem),
        ),
        scratch_shapes=[
            vmem((rows, snps), bf16),
            vmem((rows, COMP), f32),
            vmem((rows, COMP), bf16),
            vmem((COMP, rows), bf16),
            vmem((rows, COMP), f32),
            vmem((ITERS, 2, 4, 4, COMP, 128), f32),
            vmem((ITERS, 4, 4, COMP, 128), f32),
            vmem((ITERS, 4, 4, COMP, 128), f32),
            vmem((ITERS, 3, 4, COMP, 128), f32),
            vmem((ITERS, 4, COMP, 128), f32),
            vmem((ITERS, 3, COMP, 128), f32),
            vmem((ITERS, COMP, 128), f32),
            vmem((ITERS, NZ - 1, 16, 128), f32),
            vmem((ITERS, 2, 4, 4, COMP, 128), f32),
            vmem((COMP, snps), bf16),
            vmem((ITERS, COMP, COMP), f32),
            vmem((ITERS, COMP, COMP), f32),
            vmem((ITERS, 64, COMP), f32),
            vmem((ITERS, NX, 16, COMP), f32),
            vmem((ITERS, NY, 16, COMP), f32),
            vmem((ITERS, NZ, 16, COMP), f32),
            vmem((ITERS, COMP, COMP), f32),
            vmem((COMP, COMP), f32),
            vmem((COMP, COMP), f32),
            vmem((COMP, COMP), f32),
            vmem((8, 128), f32),
            pltpu.SemaphoreType.DMA((snps // SLAB,)),
            pltpu.SemaphoreType.DMA((total_copies,)),
            pltpu.SemaphoreType.DMA((total_copies,)),
        ],
        compiler_params=pltpu.CompilerParams(
            collective_id=0, has_side_effects=True
        ),
    )(
        dosage,
        keep_rows.reshape(1, n_kept),
        allele_counts.reshape(1, snps),
        projection,
    )


def solution(mesh):
    in_specs = (P(("wide", "narrow"), None), P(("wide", "narrow")), P(), P())
    out_specs = (P(("wide", "narrow"), None), P("narrow", None))
    return jax.shard_map(
        on_device, mesh=mesh, in_specs=in_specs, out_specs=out_specs, check_vma=False
    )
```
